32 devices in a mesh: seq: 16 (over z, x, core), fsdp: 2 (over y).
Axes of the slice: x: 2, y: 2, z: 4, core: 2. Of those that a mesh axis runs over, the one named last changes fastest.
Arguments:
- hidden: bfloat16 [2, 4096, 1024], P('fsdp', 'seq')
- w_qkv: bfloat16 [1024, 3072], P('fsdp')
- cond_vec: bfloat16 [1024], replicated, may hold values from -6 to 6
- head_w: bfloat16 [1024], replicated, may hold values from -0.1875 to 0.1875
- blocks: int32 [2, 64, 5], P('fsdp', 'seq'), may hold values from 0 to 63, as said below
- counts: int32 [2, 64], P('fsdp', 'seq'), may hold values from 1 to 4, 128 in all within a row
- time_idx: int32 [2, 4096], P('fsdp', 'seq'), may hold values from 0 to 999
- cond_mask: int32 [2, 4096], P('fsdp', 'seq'), may hold values 0 or 1
- noise: float32 [2, 4096], P('fsdp', 'seq'), may hold values from -6 to 6
Outputs:
- d_hidden: bfloat16 [2, 4096, 1024], P('fsdp', 'seq')
- grad_qkv: float32 [1024, 3072], P('fsdp')
The draws below stay inside these ranges and needn't reach their ends.
Inputs may be any that keep to these rules, and one draw needn't show every extreme that they name: Each list holds 5 distinct blocks of its own sequence: slot 0 is the query block itself, slot 1 a block exactly 4 blocks before or after it around the cycle of 64 blocks, and the other slots blocks within 4 of it around that cycle. Each sequence's counts sum to 128.
All inputs are finite; a program needn't handle non-finite values. No bound on the sum of `counts` or of `cond_mask` on one device may be relied on, other than what follows from the above.
Results may differ from the reference program's by a relative error of at most 0.014.
Values may be sent and summed in bfloat16 or wider, within the bound.
A program may use at most 128 MiB of HBM per device.

```python
import math
import jax
import jax.numpy as jnp
import numpy as np
from jax import lax

D = 1024
H = 16
HD = 64
BLK = 64
REACH = 4
NB = 5
STEPS = 1000
SEQS = 2
LEN = 4096
NBLK = 64


def draw_hidden(key, part):
    first = jax.random.fold_in(key, 0)
    base = jax.random.normal(first, (SEQS, LEN, D), jnp.float32)
    return base.astype(jnp.bfloat16)


def draw_w_qkv(key, part):
    first = jax.random.fold_in(key, 0)
    base = jax.random.normal(first, (D, 3 * D), jnp.float32) * D ** (-0.5)
    return base.astype(jnp.bfloat16)


def draw_blocks(key, part):
    first, second = jax.random.split(jax.random.fold_in(key, 7))
    total_rows = SEQS * NBLK
    side = jax.random.randint(first, (total_rows, 1), 0, 2, jnp.int32) * 2 - 1
    offsets_all = jnp.concatenate([jnp.arange(-REACH, 0, dtype=jnp.int32), jnp.arange(1, REACH + 1, dtype=jnp.int32)])
    ranking = jax.random.randint(second, (total_rows, 2 * REACH), 0, 65536, jnp.int32) * (2 * REACH)
    ranking = ranking + jnp.arange(2 * REACH, dtype=jnp.int32)[None, :]
    ranking = jnp.where(offsets_all[None, :] == side * REACH, -1, ranking)
    unused, picks = lax.top_k(ranking, NB - 2)
    others = offsets_all[picks]
    offsets = jnp.concatenate([jnp.zeros((total_rows, 1), jnp.int32), side * REACH, others], axis=1)
    own = jnp.tile(jnp.arange(NBLK, dtype=jnp.int32), SEQS)[:, None]
    return jnp.remainder(own + offsets, NBLK).astype(jnp.int32).reshape(SEQS, NBLK, NB)


def place_ends(entries, rng, smallest, largest):
    shape = entries.shape
    spot = [jax.random.randint(jax.random.fold_in(rng, axis), (), 0, shape[axis]) for axis in range(len(shape))]
    entries = entries.at[tuple(spot)].set(smallest)
    longest = shape.index(max(shape))
    spot[longest] = (spot[longest] + 1) % shape[longest]
    return entries.at[tuple(spot)].set(largest)


def level_of(stream_key, dims, cuts, smallest, largest):
    gain, own = 1.0, jax.random.fold_in(stream_key, 6)
    for axis_at, parts in cuts:
        steps = jnp.exp(jax.random.uniform(jax.random.fold_in(own, axis_at), (parts,), jnp.float32, smallest / len(cuts), largest / len(cuts)))
        gain = gain * jnp.repeat(steps, dims[axis_at] // parts).reshape([-1 if axis == axis_at else 1 for axis in range(len(dims))])
    return gain


def split_up(number_of, total, limit, skew):
    portions = [(1 << 20) // math.isqrt(standing ** skew) + 1 for standing in range(2, number_of + 1)]
    spare, given = total - limit - (number_of - 1), [1] * (number_of - 1)
    while spare > 0:
        free = [i for i in range(number_of - 1) if given[i] < limit]
        whole, remaining = sum([portions[i] for i in free]), spare
        for i in free:
            extra = min(limit - given[i], max(1, remaining * portions[i] // whole), spare)
            given[i] = given[i] + extra
            spare = spare - extra
    return np.array([limit] + given)


def uneven(own_key, amount, total, bound, lean):
    if amount == 2:
        one = jax.random.randint(own_key, (), max(1, total - bound), min(bound, total - 1) + 1)
        return jnp.stack([one, total - one])
    tallies = jnp.asarray(split_up(amount, total, bound, lean), jnp.int32)
    couples = (amount - 1) // 2
    donor, taker = tallies[1:1 + 2 * couples:2], tallies[2:2 + 2 * couples:2]
    margin = jnp.minimum(donor - 1, bound - taker)
    shifted = jax.random.randint(jax.random.fold_in(own_key, 1), (couples,), 0, 1 << 20) % (margin + 1)
    tallies = tallies.at[1:1 + 2 * couples:2].set(donor - shifted).at[2:2 + 2 * couples:2].set(taker + shifted)
    return tallies[jax.random.permutation(jax.random.fold_in(own_key, 2), amount)]


def scatter_about(rng, extent, spread, most, pieces=(), held_as=jnp.bfloat16):
    loudness = level_of(rng, extent, pieces, -0.22, 0.18) if pieces else 1.0
    array = jax.random.normal(rng, extent, jnp.float32) * spread * loudness
    return jnp.minimum(jnp.maximum(array, -most), most).astype(held_as)


def setup_inputs(seed: int = 0) -> dict:
    key_list = jax.random.split(jax.random.key(seed), 10)
    return {
        "hidden": draw_hidden(jax.random.fold_in(key_list[9], 71), 0),
        "w_qkv": draw_w_qkv(jax.random.fold_in(key_list[9], 71), 0),
        "cond_vec": scatter_about(key_list[2], (D,), 1.0, 6.0),
        "head_w": scatter_about(key_list[3], (D,), D ** -0.5, 0.1875),
        "blocks": draw_blocks(jax.random.fold_in(key_list[9], 71), 0),
        "counts": jax.vmap(lambda own: uneven(own, NBLK, 2 * NBLK, NB - 1, 2))(jax.random.split(key_list[5], SEQS)).reshape((SEQS, NBLK)).astype(jnp.int32),
        "time_idx": place_ends(jax.random.randint(key_list[6], (SEQS, LEN), 0, STEPS), jax.random.fold_in(key_list[6], 1), 0, STEPS - 1).astype(jnp.int32),
        "cond_mask": place_ends((jax.random.randint(key_list[7], (SEQS, LEN), 0, 3) < 1).astype(jnp.int32), jax.random.fold_in(key_list[7], 1), 0, 1),
        "noise": scatter_about(key_list[8], (SEQS, LEN), 1.0, 6.0, ((0, 2), (1, 16)), jnp.float32),
    }


EPS = 1e-05

def time_features(steps_idx, width):
    half = width // 2
    freq = jnp.exp(-math.log(10000.0) * jnp.arange(half, dtype=jnp.float32) / half)
    angle = steps_idx.astype(jnp.float32)[:, None] * freq[None, :]
    return jnp.concatenate([jnp.sin(angle), jnp.cos(angle)], axis=1)

def reference(hidden, w_qkv, cond_vec, head_w, blocks, counts, time_idx, cond_mask, noise):
    scale = HD ** (-0.5)
    cond_row = cond_vec.astype(jnp.float32)
    head_row = head_w.astype(jnp.float32)
    weights_f = w_qkv

    def one_sequence(items):
        seq_hidden, seq_blocks, seq_counts, seq_time, seq_cond, seq_noise = items
        cond = seq_cond.astype(jnp.float32)
        h_in = seq_hidden.astype(jnp.float32) + cond[:, None] * cond_row[None, :] + time_features(seq_time, D)
        inv = lax.rsqrt(lax.optimization_barrier(jnp.mean(h_in * h_in, axis=1, keepdims=True)) + EPS)
        normed = (h_in * inv).astype(jnp.bfloat16)
        qkv = jnp.dot(normed, weights_f, preferred_element_type=jnp.float32).astype(jnp.bfloat16)
        query = qkv[:, :D].reshape(NBLK, BLK, H, HD)
        pairs = qkv[:, D:].reshape(NBLK, BLK, 2 * D)
        chosen = pairs[seq_blocks].reshape(NBLK, NB * BLK, 2, H, HD)
        keys = chosen[:, :, 0]
        vals = chosen[:, :, 1]
        valid = jnp.arange(NB, dtype=jnp.int32)[None, :] <= seq_counts[:, None]
        key_valid = jnp.repeat(valid, BLK, axis=1)
        scores = jnp.einsum('tqhd,tkhd->thqk', query.astype(jnp.float32), keys.astype(jnp.float32)) * scale
        scores = jnp.where(key_valid[:, None, None, :], scores, -1e+30)
        top = lax.optimization_barrier(jnp.max(scores, axis=3, keepdims=True))
        expo = jnp.exp(scores - top)
        probs = expo / lax.optimization_barrier(jnp.sum(expo, axis=3, keepdims=True))
        probs_b = probs.astype(jnp.bfloat16)
        attn = jnp.einsum('thqk,tkhd->tqhd', probs_b.astype(jnp.float32), vals.astype(jnp.float32)).astype(jnp.bfloat16)
        h_out = h_in + attn.reshape(LEN, D).astype(jnp.float32)
        net = lax.optimization_barrier(jnp.sum(h_out * head_row[None, :], axis=1))
        d_net = 2.0 * (1.0 - cond) * (net + seq_noise)
        d_out = d_net[:, None] * head_row[None, :]
        d_attn = d_out.astype(jnp.bfloat16).reshape(NBLK, BLK, H, HD)
        delta = lax.optimization_barrier(jnp.sum(d_attn.astype(jnp.float32) * attn.astype(jnp.float32), axis=3))
        d_probs = jnp.einsum('tqhd,tkhd->thqk', d_attn.astype(jnp.float32), vals.astype(jnp.float32))
        d_scores = (probs * (d_probs - jnp.transpose(delta, (0, 2, 1))[..., None])).astype(jnp.bfloat16)
        d_query = jnp.einsum('thqk,tkhd->tqhd', d_scores.astype(jnp.float32), keys.astype(jnp.float32)) * scale
        d_keys = jnp.einsum('thqk,tqhd->tkhd', d_scores.astype(jnp.float32), query.astype(jnp.float32)) * scale
        d_vals = jnp.einsum('thqk,tqhd->tkhd', probs_b.astype(jnp.float32), d_attn.astype(jnp.float32))
        d_chosen = jnp.stack([d_keys, d_vals], axis=2).reshape(NBLK * NB, BLK, 2 * D)
        d_pairs = jnp.zeros((NBLK, BLK, 2 * D), jnp.float32).at[seq_blocks.reshape(-1)].add(d_chosen)
        d_qkv = jnp.concatenate([d_query.reshape(LEN, D), d_pairs.reshape(LEN, 2 * D)], axis=1).astype(jnp.bfloat16)
        grad = jnp.dot(normed.T, d_qkv, preferred_element_type=jnp.float32)
        d_normed = jnp.dot(d_qkv, weights_f.T, preferred_element_type=jnp.float32)
        d_in = inv * (d_normed - h_in * inv * inv * lax.optimization_barrier(jnp.mean(d_normed * h_in, axis=1, keepdims=True)))
        return ((d_out + d_in).astype(jnp.bfloat16), grad)
    d_hidden, grads = lax.map(one_sequence, (hidden, blocks, counts, time_idx, cond_mask, noise))
    return (d_hidden, lax.optimization_barrier(jnp.sum(grads, axis=0)))
```

```python
import functools
import math

import jax
import jax.numpy as jnp
from jax import lax
from jax.experimental import pallas as pl
from jax.experimental.pallas import tpu as pltpu
from jax.sharding import PartitionSpec as P

HD = 64
BLK = 64
REACH = 4
NB = 5
PAIR = 2 * HD
EPS = 1e-05
SCALE = HD ** (-0.5)
NEG = -1e30
F32 = jnp.float32
BF16 = jnp.bfloat16


def shifted(value, axis, steps):
    count = lax.axis_size(axis)
    return lax.ppermute(value, axis, [(i, (i + steps) % count) for i in range(count)])


def swapped(value, bit):
    count = lax.axis_size("seq")
    return lax.ppermute(value, "seq", [(i, i ^ bit) for i in range(count)])


def two_level():
    count = lax.axis_size("seq")
    return lax.axis_size("fsdp") == 2 and count >= 4 and count & (count - 1) == 0


def gathered(shard):
    if not two_level():
        return lax.all_gather(shard, "fsdp", axis=0, tiled=True)
    rows = shard.shape[0]
    part = rows // 4
    mine = lax.axis_index("fsdp")
    place = lax.axis_index("seq") % 4
    own = lax.dynamic_slice_in_dim(shard, place * part, part, axis=0)
    first = lax.ppermute(own, "fsdp", [(0, 1), (1, 0)])
    across = swapped(first, 2)
    pieces = ((first, 0), (across, 2), (swapped(first, 1), 1), (swapped(across, 1), 3))
    full = jnp.concatenate([shard, shard], axis=0)
    for piece, bit in pieces:
        at = (1 - mine) * rows + jnp.bitwise_xor(place, bit) * part
        full = lax.dynamic_update_slice_in_dim(full, piece, at, axis=0)
    return full


def added(a, b):
    return (a.astype(F32) + b.astype(F32)).astype(BF16)


def picked(value, index, axis=0):
    return lax.dynamic_index_in_dim(value, index, axis=axis, keepdims=False)


def reduced(grad):
    if not two_level():
        piece = lax.psum_scatter(grad, "fsdp", scatter_dimension=0, tiled=True)
        return lax.psum(piece, "seq")
    count = lax.axis_size("seq")
    bits = [1 << i for i in range(count.bit_length() - 1)]
    mine = lax.axis_index("fsdp")
    seq = lax.axis_index("seq")
    rows, cols = grad.shape
    done = []
    for chunk in jnp.split(grad, 2, axis=1):
        width = chunk.shape[1]
        halves = chunk.reshape(2, 2, rows // 4, width)
        side = seq % 2
        now = added(picked(halves, side, 1), swapped(picked(halves, 1 - side, 1), 1))
        other = lax.ppermute(picked(now, 1 - mine), "fsdp", [(0, 1), (1, 0)])
        now = added(picked(now, mine), other)
        for bit in bits[1:]:
            side = (seq // bit) % 2
            halves = now.reshape(2, now.shape[0] // 2, width)
            now = added(picked(halves, side), swapped(picked(halves, 1 - side), bit))
        for bit in bits[::-1]:
            side = (seq // bit) % 2
            got = swapped(now, bit)
            low = jnp.where(side == 0, now, got)
            high = jnp.where(side == 0, got, now)
            now = jnp.concatenate([low, high], axis=0)
        done.append(now)
    return jnp.concatenate(done, axis=1)


def time_features(steps_idx, width):
    half = width // 2
    freq = jnp.exp(-math.log(10000.0) * jnp.arange(half, dtype=F32) / half)
    angle = steps_idx.astype(F32)[:, None] * freq[None, :]
    return jnp.concatenate([jnp.sin(angle), jnp.cos(angle)], axis=1)


def dot_nt(a, b):
    return lax.dot_general(a, b, (((1,), (1,)), ((), ())), preferred_element_type=F32)


def dot_nn(a, b):
    return jnp.dot(a, b, preferred_element_type=F32)


def forward_kernel(
    heads, q_ref, k_ref, v_ref, bias_ref, h_in_ref, head_ref, cond_ref, noise_ref, stats_ref, attn_ref
):
    pair = pl.program_id(0)
    lane = lax.broadcasted_iota(jnp.int32, (1, PAIR), 1)

    @pl.when(pair == 0)
    def _():
        stats_ref[...] = jnp.zeros_like(stats_ref)

    query = q_ref[...] * jnp.asarray(SCALE, BF16)
    keys = k_ref[...]
    vals = v_ref[...]
    stats = stats_ref[...]
    outs = []
    for half in range(2):
        mine = (lane < HD) if half == 0 else (lane >= HD)
        scores = dot_nt(jnp.where(mine, query, jnp.zeros_like(query)), keys) + bias_ref[...]
        top = jnp.max(scores, axis=1, keepdims=True)
        expo = jnp.exp(scores - top)
        total = jnp.sum(expo, axis=1, keepdims=True)
        probs_b = (expo * (1.0 / total)).astype(BF16)
        outs.append(dot_nn(probs_b, vals))
        stats = jnp.where(lane == 8 * pair + half, top + jnp.log(total), stats)
    stats_ref[...] = stats
    attn_ref[pair] = jnp.where(lane < HD, outs[0], outs[1]).astype(BF16)

    @pl.when(pair == pl.num_programs(0) - 1)
    def _():
        head_row = head_ref[...]
        net = jnp.zeros_like(noise_ref[...])
        for at in range(heads // 2):
            part = slice(at * PAIR, (at + 1) * PAIR)
            h_out = h_in_ref[:, part] + attn_ref[at].astype(F32)
            net = net + jnp.sum(h_out * head_row[:, part], axis=1, keepdims=True)
        d_net = 2.0 * (1.0 - cond_ref[...]) * (net + noise_ref[...])
        full = jnp.where(lane == 4, d_net, stats_ref[...])
        for at in range(heads // 2):
            part = slice(at * PAIR, (at + 1) * PAIR)
            d_attn = (d_net * head_row[:, part]).astype(BF16).astype(F32)
            prod = d_attn * attn_ref[at].astype(F32)
            low = jnp.sum(jnp.where(lane < HD, prod, 0.0), axis=1, keepdims=True)
            high = jnp.sum(jnp.where(lane < HD, 0.0, prod), axis=1, keepdims=True)
            full = jnp.where(lane == 8 * at + 2, low, full)
            full = jnp.where(lane == 8 * at + 3, high, full)
        stats_ref[...] = full


def backward_kernel(
    q_ref, k_ref, v_ref, bias_ref, bias_t_ref, stats_ref, rows_ref, d_net_ref, head_ref, d_q_ref, d_k_ref, d_v_ref
):
    pair = pl.program_id(0)
    tokens = stats_ref.shape[0]
    lane = lax.broadcasted_iota(jnp.int32, (1, PAIR), 1)
    query = q_ref[...] * jnp.asarray(SCALE, BF16)
    keys = k_ref[...]
    vals = v_ref[...]
    own_keys = k_ref[:tokens, :]
    own_vals = v_ref[:tokens, :]
    stats = stats_ref[...]
    d_attn = (d_net_ref[...] * head_ref[...]).astype(BF16)
    d_q, d_k, d_v = [], [], []
    for half in range(2):
        mine = (lane < HD) if half == 0 else (lane >= HD)
        query_m = jnp.where(mine, query, jnp.zeros_like(query))
        d_attn_m = jnp.where(mine, d_attn, jnp.zeros_like(d_attn))
        lse = jnp.sum(jnp.where(lane == 8 * pair + half, stats, 0.0), axis=1, keepdims=True)
        delta = jnp.sum(jnp.where(lane == 8 * pair + 2 + half, stats, 0.0), axis=1, keepdims=True)
        probs = jnp.exp(dot_nt(query_m[:tokens], keys) + bias_ref[...] - lse)
        d_probs = dot_nt(d_attn_m[:tokens], vals)
        d_scores = (probs * (d_probs - delta)).astype(BF16)
        d_q.append(dot_nn(d_scores, keys))
        lse_row = rows_ref[half : half + 1, :]
        delta_row = rows_ref[2 + half : 3 + half, :]
        probs_t = jnp.exp(dot_nt(own_keys, query_m) + bias_t_ref[...] - lse_row)
        d_v.append(dot_nn(probs_t.astype(BF16), d_attn))
        d_probs_t = dot_nt(own_vals, d_attn_m)
        d_scores_t = (probs_t * (d_probs_t - delta_row)).astype(BF16)
        d_k.append(dot_nn(d_scores_t, query))
    low = lane < HD
    d_q_ref[...] = (jnp.where(low, d_q[0], d_q[1]) * SCALE).astype(BF16)
    d_k_ref[...] = jnp.where(low, d_k[0], d_k[1]).astype(BF16)
    d_v_ref[...] = jnp.where(low, d_v[0], d_v[1]).astype(BF16)


def whole(shape):
    return pl.BlockSpec(shape, lambda pair: (0, 0))


def forward_call(qkv, bias, h_in, head_row, cond, noise):
    ext = qkv.shape[0]
    tokens, width = h_in.shape
    pairs = width // PAIR
    return pl.pallas_call(
        functools.partial(forward_kernel, width // HD),
        grid=(pairs,),
        in_specs=[
            pl.BlockSpec((tokens, PAIR), lambda pair: (0, pair)),
            pl.BlockSpec((ext, PAIR), lambda pair: (0, pairs + pair)),
            pl.BlockSpec((ext, PAIR), lambda pair: (0, 2 * pairs + pair)),
            whole((tokens, ext)),
            whole((tokens, width)),
            whole((1, width)),
            whole((tokens, 1)),
            whole((tokens, 1)),
        ],
        out_specs=whole((tokens, PAIR)),
        out_shape=jax.ShapeDtypeStruct((tokens, PAIR), F32),
        scratch_shapes=[pltpu.VMEM((pairs, tokens, PAIR), BF16)],
        compiler_params=pltpu.CompilerParams(vmem_limit_bytes=40 << 20),
        name="attn_forward",
    )(qkv, qkv, qkv, bias, h_in, head_row, cond, noise)


def backward_call(qkv, bias, bias_t, stats, rows, d_net, head_row):
    ext = qkv.shape[0]
    tokens = stats.shape[0]
    width = head_row.shape[1]
    pairs = width // PAIR
    return pl.pallas_call(
        backward_kernel,
        grid=(pairs,),
        in_specs=[
            pl.BlockSpec((ext, PAIR), lambda pair: (0, pair)),
            pl.BlockSpec((ext, PAIR), lambda pair: (0, pairs + pair)),
            pl.BlockSpec((ext, PAIR), lambda pair: (0, 2 * pairs + pair)),
            whole((tokens, ext)),
            whole((tokens, ext)),
            whole((tokens, PAIR)),
            pl.BlockSpec((8, ext), lambda pair: (pair, 0)),
            whole((ext, 1)),
            pl.BlockSpec((1, PAIR), lambda pair: (0, pair)),
        ],
        out_specs=[pl.BlockSpec((tokens, PAIR), lambda pair: (0, pair))] * 3,
        out_shape=[jax.ShapeDtypeStruct((tokens, width), BF16)] * 3,
        compiler_params=pltpu.CompilerParams(vmem_limit_bytes=48 << 20),
        name="attn_backward",
    )(qkv, qkv, qkv, bias, bias_t, stats, rows, d_net, head_row)


def body(hidden, w_qkv, cond_vec, head_w, blocks, counts, time_idx, cond_mask, noise):
    tokens = hidden.shape[1]
    width = hidden.shape[2]
    heads = width // HD
    local_blocks = tokens // BLK
    halo = REACH * BLK
    blocks_all = local_blocks * lax.axis_size("seq")
    first_block = lax.axis_index("seq") * local_blocks

    used = lax.broadcasted_iota(jnp.int32, (local_blocks, NB), 1) <= counts[0][:, None]
    listed = jnp.where(used, blocks[0], -1)
    listed_ext = jnp.concatenate(
        [
            listed,
            shifted(listed[local_blocks - REACH :], "seq", 1),
            shifted(listed[:REACH], "seq", -1),
        ],
        axis=0,
    )
    own_ids = first_block + jnp.arange(local_blocks, dtype=jnp.int32)
    left_ids = first_block - REACH + jnp.arange(REACH, dtype=jnp.int32)
    right_ids = first_block + local_blocks + jnp.arange(REACH, dtype=jnp.int32)
    ext_ids = jnp.remainder(jnp.concatenate([own_ids, left_ids, right_ids]), blocks_all)

    def bias_of(seen):
        seen = jnp.repeat(jnp.repeat(seen, BLK, axis=0), BLK, axis=1)
        return jnp.where(seen, 0.0, NEG).astype(F32)

    bias = bias_of(jnp.any(listed[:, None, :] == ext_ids[None, :, None], axis=2))
    bias_t = bias_of(jnp.any(listed_ext[None, :, :] == own_ids[:, None, None], axis=2))

    cond = cond_mask[0].astype(F32)[:, None]
    head_row = head_w.astype(F32)[None, :]
    h_in = (
        hidden[0].astype(F32)
        + cond * cond_vec.astype(F32)[None, :]
        + time_features(time_idx[0], width)
    )
    inv = lax.rsqrt(jnp.mean(h_in * h_in, axis=1, keepdims=True) + EPS)
    normed = (h_in * inv).astype(BF16)
    normed_ext = jnp.concatenate(
        [
            normed,
            shifted(normed[tokens - halo :], "seq", 1),
            shifted(normed[:halo], "seq", -1),
        ],
        axis=0,
    )
    weights = gathered(w_qkv)
    qkv = jnp.dot(normed_ext, weights, preferred_element_type=F32).astype(BF16)

    stats = forward_call(qkv, bias, h_in, head_row, cond, noise[0][:, None])
    rows = stats[:, : 4 * heads].T
    rows_ext = jnp.concatenate(
        [
            rows,
            shifted(rows[:, tokens - halo :], "seq", 1),
            shifted(rows[:, :halo], "seq", -1),
        ],
        axis=1,
    )
    d_net_ext = rows_ext[4][:, None]
    d_qkv = jnp.concatenate(
        backward_call(qkv, bias, bias_t, stats, rows_ext, d_net_ext, head_row), axis=1
    )

    partial_grad = jnp.einsum("tc,tk->ck", normed, d_qkv, preferred_element_type=F32).astype(BF16)
    grad = reduced(partial_grad).astype(F32)
    d_normed = lax.dot_general(
        d_qkv, weights, (((1,), (1,)), ((), ())), preferred_element_type=F32
    )
    d_out = stats[:, 4:5] * head_row
    d_in = inv * (d_normed - h_in * inv * inv * jnp.mean(d_normed * h_in, axis=1, keepdims=True))
    d_hidden = (d_out + d_in).astype(BF16)
    return (d_hidden[None], grad)


def solution(mesh):
    return jax.shard_map(
        body,
        mesh=mesh,
        in_specs=(
            P("fsdp", "seq", None),
            P("fsdp", None),
            P(),
            P(),
            P("fsdp", "seq", None),
            P("fsdp", "seq"),
            P("fsdp", "seq"),
            P("fsdp", "seq"),
            P("fsdp", "seq"),
        ),
        out_specs=(P("fsdp", "seq", None), P("fsdp", None)),
        check_vma=False,
    )
```

```python
import functools
import math

import jax
import jax.numpy as jnp
from jax import lax
from jax.experimental import pallas as pl
from jax.experimental.pallas import tpu as pltpu
from jax.sharding import PartitionSpec as P

HD = 64
BLK = 64
REACH = 4
NB = 5
PAIR = 2 * HD
EPS = 1e-05
SCALE = HD ** (-0.5)
NEG = -1e30
F32 = jnp.float32
BF16 = jnp.bfloat16


def shifted(value, axis, steps):
    count = lax.axis_size(axis)
    return lax.ppermute(value, axis, [(i, (i + steps) % count) for i in range(count)])


def swapped(value, bit):
    count = lax.axis_size("seq")
    return lax.ppermute(value, "seq", [(i, i ^ bit) for i in range(count)])


def two_level():
    count = lax.axis_size("seq")
    return lax.axis_size("fsdp") == 2 and count >= 4 and count & (count - 1) == 0


def gathered(shard):
    if not two_level():
        return lax.all_gather(shard, "fsdp", axis=0, tiled=True)
    rows = shard.shape[0]
    part = rows // 4
    mine = lax.axis_index("fsdp")
    place = lax.axis_index("seq") % 4
    own = lax.dynamic_slice_in_dim(shard, place * part, part, axis=0)
    first = lax.ppermute(own, "fsdp", [(0, 1), (1, 0)])
    across = swapped(first, 2)
    pieces = ((first, 0), (across, 2), (swapped(first, 1), 1), (swapped(across, 1), 3))
    full = jnp.concatenate([shard, shard], axis=0)
    for piece, bit in pieces:
        at = (1 - mine) * rows + jnp.bitwise_xor(place, bit) * part
        full = lax.dynamic_update_slice_in_dim(full, piece, at, axis=0)
    return full


def added(a, b):
    return (a.astype(F32) + b.astype(F32)).astype(BF16)


def picked(value, index, axis=0):
    return lax.dynamic_index_in_dim(value, index, axis=axis, keepdims=False)


def reduced(grad):
    if not two_level():
        piece = lax.psum_scatter(grad, "fsdp", scatter_dimension=0, tiled=True)
        return lax.psum(piece, "seq")
    count = lax.axis_size("seq")
    bits = [1 << i for i in range(count.bit_length() - 1)]
    mine = lax.axis_index("fsdp")
    seq = lax.axis_index("seq")
    rows = grad.shape[0] // 2
    done = []
    for at, chunk in enumerate(jnp.split(grad, 2, axis=1)):
        width = chunk.shape[1]
        now = chunk.reshape(2, rows, width)
        for step, bit in enumerate(bits):
            if step == 1 + at:
                other = lax.ppermute(picked(now, 1 - mine), "fsdp", [(0, 1), (1, 0)])
                now = added(picked(now, mine), other)
            lead = now.ndim - 2
            side = (seq // bit) % 2
            halves = now.reshape(now.shape[:lead] + (2, now.shape[lead] // 2, width))
            sent = swapped(picked(halves, 1 - side, lead), bit)
            now = added(picked(halves, side, lead), sent)
        if now.ndim == 3:
            other = lax.ppermute(picked(now, 1 - mine), "fsdp", [(0, 1), (1, 0)])
            now = added(picked(now, mine), other)
        for bit in bits[:0:-1]:
            side = (seq // bit) % 2
            got = swapped(now, bit)
            low = jnp.where(side == 0, now, got)
            high = jnp.where(side == 0, got, now)
            now = jnp.concatenate([low, high], axis=0)
        done += [now, swapped(now, 1)]
    return joined(seq % 2, done)


def join_kernel(side_ref, own_0, got_0, own_1, got_1, out_ref):
    mine = pl.program_id(0) == side_ref[0]
    width = own_0.shape[1]

    @pl.when(mine)
    def _():
        out_ref[:, :width] = own_0[...].astype(F32)
        out_ref[:, width:] = own_1[...].astype(F32)

    @pl.when(jnp.logical_not(mine))
    def _():
        out_ref[:, :width] = got_0[...].astype(F32)
        out_ref[:, width:] = got_1[...].astype(F32)


def joined(side, parts):
    rows, width = parts[0].shape
    tile = min(rows, 64)
    tiles = rows // tile
    return pl.pallas_call(
        join_kernel,
        grid=(2, tiles),
        in_specs=[pl.BlockSpec(memory_space=pltpu.SMEM)]
        + [pl.BlockSpec((tile, width), lambda half, at: (at, 0))] * 4,
        out_specs=pl.BlockSpec((tile, 2 * width), lambda half, at: (half * tiles + at, 0)),
        out_shape=jax.ShapeDtypeStruct((2 * rows, 2 * width), F32),
        compiler_params=pltpu.CompilerParams(vmem_limit_bytes=32 << 20),
        name="join_halves",
    )(side.astype(jnp.int32).reshape(1), *parts)


def time_features(steps_idx, width):
    half = width // 2
    freq = jnp.exp(-math.log(10000.0) * jnp.arange(half, dtype=F32) / half)
    angle = steps_idx.astype(F32)[:, None] * freq[None, :]
    return jnp.concatenate([jnp.sin(angle), jnp.cos(angle)], axis=1)


def dot_nt(a, b):
    return lax.dot_general(a, b, (((1,), (1,)), ((), ())), preferred_element_type=F32)


def dot_nn(a, b):
    return jnp.dot(a, b, preferred_element_type=F32)


def forward_kernel(
    heads, q_ref, k_ref, v_ref, bias_ref, h_in_ref, head_ref, cond_ref, noise_ref, stats_ref, attn_ref
):
    pair = pl.program_id(0)
    lane = lax.broadcasted_iota(jnp.int32, (1, PAIR), 1)

    @pl.when(pair == 0)
    def _():
        stats_ref[...] = jnp.zeros_like(stats_ref)

    query = q_ref[...] * jnp.asarray(SCALE, BF16)
    keys = k_ref[...]
    vals = v_ref[...]
    stats = stats_ref[...]
    outs = []
    for half in range(2):
        mine = (lane < HD) if half == 0 else (lane >= HD)
        scores = dot_nt(jnp.where(mine, query, jnp.zeros_like(query)), keys) + bias_ref[...]
        top = jnp.max(scores, axis=1, keepdims=True)
        expo = jnp.exp(scores - top)
        total = jnp.sum(expo, axis=1, keepdims=True)
        probs_b = (expo * (1.0 / total)).astype(BF16)
        outs.append(dot_nn(probs_b, vals))
        stats = jnp.where(lane == 8 * pair + half, top + jnp.log(total), stats)
    stats_ref[...] = stats
    attn_ref[pair] = jnp.where(lane < HD, outs[0], outs[1]).astype(BF16)

    @pl.when(pair == pl.num_programs(0) - 1)
    def _():
        head_row = head_ref[...]
        net = jnp.zeros_like(noise_ref[...])
        for at in range(heads // 2):
            part = slice(at * PAIR, (at + 1) * PAIR)
            h_out = h_in_ref[:, part] + attn_ref[at].astype(F32)
            net = net + jnp.sum(h_out * head_row[:, part], axis=1, keepdims=True)
        d_net = 2.0 * (1.0 - cond_ref[...]) * (net + noise_ref[...])
        full = jnp.where(lane == 4, d_net, stats_ref[...])
        for at in range(heads // 2):
            part = slice(at * PAIR, (at + 1) * PAIR)
            d_attn = (d_net * head_row[:, part]).astype(BF16).astype(F32)
            prod = d_attn * attn_ref[at].astype(F32)
            low = jnp.sum(jnp.where(lane < HD, prod, 0.0), axis=1, keepdims=True)
            high = jnp.sum(jnp.where(lane < HD, 0.0, prod), axis=1, keepdims=True)
            full = jnp.where(lane == 8 * at + 2, low, full)
            full = jnp.where(lane == 8 * at + 3, high, full)
        stats_ref[...] = full


def backward_kernel(
    q_ref, k_ref, v_ref, bias_ref, bias_t_ref, stats_ref, rows_ref, d_net_ref, head_ref, d_q_ref, d_k_ref, d_v_ref
):
    pair = pl.program_id(0)
    tokens = stats_ref.shape[0]
    lane = lax.broadcasted_iota(jnp.int32, (1, PAIR), 1)
    query = q_ref[...] * jnp.asarray(SCALE, BF16)
    keys = k_ref[...]
    vals = v_ref[...]
    own_keys = k_ref[:tokens, :]
    own_vals = v_ref[:tokens, :]
    stats = stats_ref[...]
    d_attn = (d_net_ref[...] * head_ref[...]).astype(BF16)
    d_q, d_k, d_v = [], [], []
    for half in range(2):
        mine = (lane < HD) if half == 0 else (lane >= HD)
        query_m = jnp.where(mine, query, jnp.zeros_like(query))
        d_attn_m = jnp.where(mine, d_attn, jnp.zeros_like(d_attn))
        lse = jnp.sum(jnp.where(lane == 8 * pair + half, stats, 0.0), axis=1, keepdims=True)
        delta = jnp.sum(jnp.where(lane == 8 * pair + 2 + half, stats, 0.0), axis=1, keepdims=True)
        probs = jnp.exp(dot_nt(query_m[:tokens], keys) + bias_ref[...] - lse)
        d_probs = dot_nt(d_attn_m[:tokens], vals)
        d_scores = (probs * (d_probs - delta)).astype(BF16)
        d_q.append(dot_nn(d_scores, keys))
        lse_row = rows_ref[half : half + 1, :]
        delta_row = rows_ref[2 + half : 3 + half, :]
        probs_t = jnp.exp(dot_nt(own_keys, query_m) + bias_t_ref[...] - lse_row)
        d_v.append(dot_nn(probs_t.astype(BF16), d_attn))
        d_probs_t = dot_nt(own_vals, d_attn_m)
        d_scores_t = (probs_t * (d_probs_t - delta_row)).astype(BF16)
        d_k.append(dot_nn(d_scores_t, query))
    low = lane < HD
    d_q_ref[...] = (jnp.where(low, d_q[0], d_q[1]) * SCALE).astype(BF16)
    d_k_ref[...] = jnp.where(low, d_k[0], d_k[1]).astype(BF16)
    d_v_ref[...] = jnp.where(low, d_v[0], d_v[1]).astype(BF16)


def whole(shape):
    return pl.BlockSpec(shape, lambda pair: (0, 0))


def forward_call(qkv, bias, h_in, head_row, cond, noise):
    ext = qkv.shape[0]
    tokens, width = h_in.shape
    pairs = width // PAIR
    return pl.pallas_call(
        functools.partial(forward_kernel, width // HD),
        grid=(pairs,),
        in_specs=[
            pl.BlockSpec((tokens, PAIR), lambda pair: (0, pair)),
            pl.BlockSpec((ext, PAIR), lambda pair: (0, pairs + pair)),
            pl.BlockSpec((ext, PAIR), lambda pair: (0, 2 * pairs + pair)),
            whole((tokens, ext)),
            whole((tokens, width)),
            whole((1, width)),
            whole((tokens, 1)),
            whole((tokens, 1)),
        ],
        out_specs=whole((tokens, PAIR)),
        out_shape=jax.ShapeDtypeStruct((tokens, PAIR), F32),
        scratch_shapes=[pltpu.VMEM((pairs, tokens, PAIR), BF16)],
        compiler_params=pltpu.CompilerParams(vmem_limit_bytes=40 << 20),
        name="attn_forward",
    )(qkv, qkv, qkv, bias, h_in, head_row, cond, noise)


def backward_call(qkv, bias, bias_t, stats, rows, d_net, head_row):
    ext = qkv.shape[0]
    tokens = stats.shape[0]
    width = head_row.shape[1]
    pairs = width // PAIR
    return pl.pallas_call(
        backward_kernel,
        grid=(pairs,),
        in_specs=[
            pl.BlockSpec((ext, PAIR), lambda pair: (0, pair)),
            pl.BlockSpec((ext, PAIR), lambda pair: (0, pairs + pair)),
            pl.BlockSpec((ext, PAIR), lambda pair: (0, 2 * pairs + pair)),
            whole((tokens, ext)),
            whole((tokens, ext)),
            whole((tokens, PAIR)),
            pl.BlockSpec((8, ext), lambda pair: (pair, 0)),
            whole((ext, 1)),
            pl.BlockSpec((1, PAIR), lambda pair: (0, pair)),
        ],
        out_specs=[pl.BlockSpec((tokens, PAIR), lambda pair: (0, pair))] * 3,
        out_shape=[jax.ShapeDtypeStruct((tokens, width), BF16)] * 3,
        compiler_params=pltpu.CompilerParams(vmem_limit_bytes=48 << 20),
        name="attn_backward",
    )(qkv, qkv, qkv, bias, bias_t, stats, rows, d_net, head_row)


def body(hidden, w_qkv, cond_vec, head_w, blocks, counts, time_idx, cond_mask, noise):
    tokens = hidden.shape[1]
    width = hidden.shape[2]
    heads = width // HD
    local_blocks = tokens // BLK
    halo = REACH * BLK
    blocks_all = local_blocks * lax.axis_size("seq")
    first_block = lax.axis_index("seq") * local_blocks

    used = lax.broadcasted_iota(jnp.int32, (local_blocks, NB), 1) <= counts[0][:, None]
    listed = jnp.where(used, blocks[0], -1)
    listed_ext = jnp.concatenate(
        [
            listed,
            shifted(listed[local_blocks - REACH :], "seq", 1),
            shifted(listed[:REACH], "seq", -1),
        ],
        axis=0,
    )
    own_ids = first_block + jnp.arange(local_blocks, dtype=jnp.int32)
    left_ids = first_block - REACH + jnp.arange(REACH, dtype=jnp.int32)
    right_ids = first_block + local_blocks + jnp.arange(REACH, dtype=jnp.int32)
    ext_ids = jnp.remainder(jnp.concatenate([own_ids, left_ids, right_ids]), blocks_all)

    def bias_of(seen):
        seen = jnp.repeat(jnp.repeat(seen, BLK, axis=0), BLK, axis=1)
        return jnp.where(seen, 0.0, NEG).astype(F32)

    bias = bias_of(jnp.any(listed[:, None, :] == ext_ids[None, :, None], axis=2))
    bias_t = bias_of(jnp.any(listed_ext[None, :, :] == own_ids[:, None, None], axis=2))

    cond = cond_mask[0].astype(F32)[:, None]
    head_row = head_w.astype(F32)[None, :]
    h_in = (
        hidden[0].astype(F32)
        + cond * cond_vec.astype(F32)[None, :]
        + time_features(time_idx[0], width)
    )
    inv = lax.rsqrt(jnp.mean(h_in * h_in, axis=1, keepdims=True) + EPS)
    normed = (h_in * inv).astype(BF16)
    normed_ext = jnp.concatenate(
        [
            normed,
            shifted(normed[tokens - halo :], "seq", 1),
            shifted(normed[:halo], "seq", -1),
        ],
        axis=0,
    )
    weights = gathered(w_qkv)
    qkv = jnp.dot(normed_ext, weights, preferred_element_type=F32).astype(BF16)

    stats = forward_call(qkv, bias, h_in, head_row, cond, noise[0][:, None])
    rows = stats[:, : 4 * heads].T
    rows_ext = jnp.concatenate(
        [
            rows,
            shifted(rows[:, tokens - halo :], "seq", 1),
            shifted(rows[:, :halo], "seq", -1),
        ],
        axis=1,
    )
    d_net_ext = rows_ext[4][:, None]
    d_qkv = jnp.concatenate(
        backward_call(qkv, bias, bias_t, stats, rows_ext, d_net_ext, head_row), axis=1
    )

    partial_grad = jnp.einsum("tc,tk->ck", normed, d_qkv, preferred_element_type=F32).astype(BF16)
    grad = reduced(partial_grad).astype(F32)
    d_normed = lax.dot_general(
        d_qkv, weights, (((1,), (1,)), ((), ())), preferred_element_type=F32
    )
    d_out = stats[:, 4:5] * head_row
    d_in = inv * (d_normed - h_in * inv * inv * jnp.mean(d_normed * h_in, axis=1, keepdims=True))
    d_hidden = (d_out + d_in).astype(BF16)
    return (d_hidden[None], grad)


def solution(mesh):
    return jax.shard_map(
        body,
        mesh=mesh,
        in_specs=(
            P("fsdp", "seq", None),
            P("fsdp", None),
            P(),
            P(),
            P("fsdp", "seq", None),
            P("fsdp", "seq"),
            P("fsdp", "seq"),
            P("fsdp", "seq"),
            P("fsdp", "seq"),
        ),
        out_specs=(P("fsdp", "seq", None), P("fsdp", None)),
        check_vma=False,
    )
```
